32 devices in a mesh: parts: 2 (over y), seq: 8 (over z, x), head: 2 (over core).
Axes of the slice: x: 2, y: 2, z: 4, core: 2. Of those that a mesh axis runs over, the one named last changes fastest.
Arguments:
- query_states: bfloat16 [4096, 8192], P(('parts', 'seq', 'head')), parts along dimension 0, may hold values from -80 to 80, as said below
- key_states: bfloat16 [4096, 1024], P(('parts', 'seq', 'head')), parts along dimension 0, may hold values from -6 to 6
- value_states: bfloat16 [4096, 1024], P(('parts', 'seq', 'head')), parts along dimension 0, may hold values from -12 to 12
- vertical_blocks: int32 [16, 6], P('parts'), parts along dimension 0, may hold values from 0 to 31, as said below
- slash_offsets: int32 [16, 6], P('parts'), parts along dimension 0, may hold values from 0 to 7, as said below
Outputs:
- attended: bfloat16 [4096, 8192], P(('parts', 'seq', 'head')), parts along dimension 0
The draws below stay inside these ranges and needn't reach their ends.
There are 2 independent parts, one for each index of `parts`. The reference program is written for one: setup_inputs(seed, part) draws one part's arguments, and reference() takes and returns one part's arrays. A program takes and returns all parts, laid end to end along the dimension named above; each array names one. Nothing has to cross between parts.
Inputs may be any that keep to these rules, and one draw needn't show every extreme that they name: `query_states`: entries of order one, a few larger. `vertical_blocks`: each row lists 6 different key blocks, among them block 0. `slash_offsets`: each row lists 6 different block offsets, among them 0 and 1.
All inputs are finite; a program needn't handle non-finite values.
Results may differ from the reference program's by a relative error of at most 0.0034.
Values may be sent and summed in bfloat16 or wider, within the bound.
No kernel may reach another device: no remote copies, remote signals or barrier semaphores. Data moves between devices by JAX's collectives and lax.ppermute only.
A program may use at most 64 MiB of HBM per device.

```python
import math
import jax
import jax.numpy as jnp
from jax import lax

QH = 64
KVH = 8
HD = 128
TOK_DEV = 256
BS = 64
NS = 6
NV = 6
S = 2048
QB = 32
SPAN = 8


def draw_states(key):
    folded = jax.random.fold_in(key, 7)
    key_stream, query_stream = jax.random.split(folded)
    groups = QH // KVH
    key_field = jnp.clip(jax.random.normal(key_stream, (S, KVH, HD), jnp.float32), -6.0, 6.0)
    query_field = jnp.clip(2.0 * jax.random.normal(query_stream, (S, KVH, groups, HD), jnp.float32), -12.0, 12.0)
    query_field = jnp.clip(query_field, -80.0, 80.0)
    return (query_field.reshape(S, QH * HD), jnp.clip(key_field, -6.0, 6.0).reshape(S, KVH * HD))


def draw_query_states(key, part):
    return draw_states(key)[0].astype(jnp.bfloat16)


def draw_key_states(key, part):
    return draw_states(key)[1].astype(jnp.bfloat16)


def draw_vertical_blocks(key, part):
    folded = jax.random.fold_in(key, 11)
    streams = jax.random.split(folded, KVH)

    def per_head(stream):
        chosen = jax.random.permutation(stream, QB - 2)[:NV - 2] + 1
        return jnp.concatenate([jnp.array([0, QB - 1], jnp.int32), chosen.astype(jnp.int32)])
    return jax.vmap(per_head)(streams)


def draw_slash_offsets(key, part):
    folded = jax.random.fold_in(key, 13)
    streams = jax.random.split(folded, KVH)

    def per_head(stream):
        chosen = jax.random.permutation(stream, SPAN - 3)[:NS - 3] + 2
        return jnp.concatenate([jnp.array([0, 1, SPAN - 1], jnp.int32), chosen.astype(jnp.int32)])
    return jax.vmap(per_head)(streams)


def block_scale(rng, shape, shards, least, top_value):
    gain, own = 1.0, jax.random.fold_in(rng, 6)
    for dim, parts in shards:
        draws = jnp.exp(jax.random.uniform(jax.random.fold_in(own, dim), (parts,), jnp.float32, least / len(shards), top_value / len(shards)))
        gain = gain * jnp.repeat(draws, shape[dim] // parts).reshape([-1 if axis == dim else 1 for axis in range(len(shape))])
    return gain


def bell_draw(stream_key, shape, deviation, most, shards=(), kind=jnp.bfloat16):
    values = deviation * jax.random.normal(stream_key, shape, jnp.float32)
    if shards:
        values = values * block_scale(stream_key, shape, shards, -0.22, 0.18)
    return jnp.clip(values, -most, most).astype(kind)


def setup_inputs(seed: int = 0, part: int = 0) -> dict:
    key_list = jax.random.split(jax.random.key(seed), 6)
    part_splits = jax.random.split(jax.random.fold_in(key_list[5], part), 6)
    query_states = draw_query_states(jax.random.fold_in(jax.random.fold_in(key_list[5], part), 71), part)
    key_states = draw_key_states(jax.random.fold_in(jax.random.fold_in(key_list[5], part), 71), part)
    value_states = bell_draw(part_splits[2], (S, KVH * HD), 2.0, 12.0, ((0, 16),))
    vertical_blocks = draw_vertical_blocks(jax.random.fold_in(jax.random.fold_in(key_list[5], part), 71), part)
    slash_offsets = draw_slash_offsets(jax.random.fold_in(jax.random.fold_in(key_list[5], part), 71), part)
    return {"query_states": query_states, "key_states": key_states, "value_states": value_states, "vertical_blocks": vertical_blocks, "slash_offsets": slash_offsets}


def block_mask(query_block, slash_here, vertical_here):
    positions = jnp.arange(BS, dtype=jnp.int32)
    causal = positions[None, :] <= positions[:, None]
    key_block = query_block - slash_here
    slash_ok = (key_block >= 0)[:, :, None, None] & ((slash_here != 0)[:, :, None, None] | causal[None, None])
    slash_ok = jnp.transpose(slash_ok, (0, 2, 1, 3)).reshape(slash_here.shape[0], BS, -1)
    on_slash = jnp.any((query_block - vertical_here)[:, :, None] == slash_here[:, None, :], axis=-1)
    vertical_ok = (vertical_here <= query_block) & jnp.logical_not(on_slash)
    vertical_ok = jnp.broadcast_to(vertical_ok[:, None, :, None], (vertical_here.shape[0], BS, vertical_here.shape[1], BS))
    vertical_ok = vertical_ok.reshape(vertical_here.shape[0], BS, -1)
    return jnp.concatenate([slash_ok, vertical_ok], axis=-1)

def attend_block(query_tile, key_rows, value_rows, active, score_scale):
    scores = jnp.einsum('tgch,gkh->gctk', query_tile.astype(jnp.float32), key_rows.astype(jnp.float32)) * score_scale
    scores = jnp.where(active[:, None], scores, -jnp.inf)
    row_max = lax.optimization_barrier(jnp.max(scores, axis=-1, keepdims=True))
    weights = jnp.exp(scores - row_max)
    row_total = lax.optimization_barrier(jnp.sum(weights, axis=-1))
    rounded = weights.astype(jnp.bfloat16)
    mixed_rows = jnp.einsum('gctk,gkh->tgch', rounded.astype(jnp.float32), value_rows.astype(jnp.float32))
    mixed_rows = mixed_rows / jnp.transpose(row_total, (2, 0, 1))[..., None]
    return mixed_rows.astype(jnp.bfloat16)

def reference(query_states, key_states, value_states, vertical_blocks, slash_offsets):
    groups = QH // KVH
    query_blocks = query_states.reshape(QB, BS, KVH, groups, HD)
    key_blocks = key_states.reshape(QB, BS, KVH, HD)
    value_blocks = value_states.reshape(QB, BS, KVH, HD)
    head_rows = jnp.arange(KVH, dtype=jnp.int32)[:, None]
    score_scale = 1.0 / math.sqrt(HD)

    def one_block(query_block):
        nearby = jnp.clip(query_block - slash_offsets, 0, QB - 1).astype(jnp.int32)
        key_rows = jnp.concatenate([key_blocks[nearby, :, head_rows, :], key_blocks[vertical_blocks, :, head_rows, :]], axis=1)
        value_rows = jnp.concatenate([value_blocks[nearby, :, head_rows, :], value_blocks[vertical_blocks, :, head_rows, :]], axis=1)
        key_rows = key_rows.reshape(KVH, -1, HD)
        value_rows = value_rows.reshape(KVH, -1, HD)
        active = block_mask(query_block, slash_offsets, vertical_blocks)
        return attend_block(query_blocks[query_block], key_rows, value_rows, active, score_scale)

    def block_group(block_ids):
        return jax.vmap(one_block)(block_ids)
    block_ids = jnp.arange(QB, dtype=jnp.int32).reshape(-1, TOK_DEV // BS)
    mixed_rows = lax.map(block_group, block_ids)
    return mixed_rows.reshape(S, QH * HD)
```

```python
import functools
import math

import jax
import jax.numpy as jnp
from jax import lax
from jax.experimental import pallas as pl
from jax.experimental.pallas import tpu as pltpu
from jax.sharding import PartitionSpec as P

BS = 64
SPAN = 8
GATHER_BYTES = 16 * 2**20
LANES = 128


def passed_along(block, axis, distance):
    devices = range(lax.axis_size(axis))
    route = [(i - distance, i) for i in devices if i - distance in devices]
    return lax.ppermute(block, axis, route)


def swapped(block, axis):
    return lax.ppermute(block, axis, [(i, i ^ 1) for i in range(lax.axis_size(axis))])


def head_scores(query, keys):
    return lax.dot_general(
        query, keys, (((1,), (1,)), ((), ())), preferred_element_type=jnp.float32
    )


def attend_kernel(cfg, *refs):
    pieces, first, where, near, last = cfg
    vert_ref, slash_ref, q_ref = refs[:3]
    refs = refs[3:]
    key_pieces, value_pieces = refs[:pieces], refs[pieces : 2 * pieces]
    refs = refs[2 * pieces :]
    if near:
        out_ref, lse_ref = refs[:2]
        refs = refs[2:]
    else:
        prev_ref, prev_lse_ref, out_ref = refs[:3]
        refs = refs[3:]
    keys, values, sems = refs
    head, heads = pl.program_id(0), pl.num_programs(0)
    rows = key_pieces[0].shape[0]
    slots = keys.shape[1] // BS
    head_dim = keys.shape[2]
    groups = q_ref.shape[1] // head_dim
    blocks = q_ref.shape[0] // BS
    offsets = slash_ref.shape[1]
    columns = vert_ref.shape[1]
    position = lax.axis_index("seq") * lax.axis_size("head") + lax.axis_index("head")
    places = where()
    first_block = first()

    def fetch(at, slot):
        lanes = pl.ds(pl.multiple_of(at * head_dim, head_dim), head_dim)
        for piece in range(pieces):
            to = pl.ds(pl.multiple_of(places[piece] * rows, rows), rows)
            pltpu.make_async_copy(
                key_pieces[piece].at[:, lanes], keys.at[slot, to], sems.at[0, slot]
            ).start()
            pltpu.make_async_copy(
                value_pieces[piece].at[:, lanes], values.at[slot, to], sems.at[1, slot]
            ).start()

    now = lax.rem(head, 2)

    @pl.when(head == 0)
    def _():
        fetch(head, now)

    @pl.when(head + 1 < heads)
    def _():
        fetch(head + 1, 1 - now)

    pltpu.make_async_copy(keys.at[now], keys.at[now], sems.at[0, now]).wait()
    pltpu.make_async_copy(values.at[now], values.at[now], sems.at[1, now]).wait()

    factor = math.log2(math.e) / math.sqrt(head_dim)
    lane = lax.broadcasted_iota(jnp.int32, (1, BS), 1)
    zero, minus = jnp.float32(0), jnp.float32(-jnp.inf)
    for b in range(blocks):
        block = position * blocks + b
        picked, bias = [], []
        if near:
            spare = slash_ref[head, 0]
            for m in range(offsets):
                if m == 0:
                    offset = jnp.int32(0)
                else:
                    offset = slash_ref[head, m]
                    offset = jnp.where(offset == 0, spare, offset)
                wanted = block - offset
                picked.append(jnp.clip(wanted - first_block, 0, slots - 1))
                bias.append(jnp.where(wanted >= 0, zero, minus))
        else:
            for m in range(columns):
                wanted = vert_ref[head, m]
                used = wanted <= block
                for n in range(offsets):
                    used = used & (block - wanted != slash_ref[head, n])
                at = m if first_block is None else wanted - first_block
                picked.append(jnp.clip(at, 0, slots - 1))
                bias.append(jnp.where(used, zero, minus))
        spans = [pl.ds(pl.multiple_of(at * BS, BS), BS) for at in picked]
        block_keys = jnp.concatenate([keys[now, s] for s in spans], axis=0)
        block_values = jnp.concatenate([values[now, s] for s in spans], axis=0)
        bias_row = jnp.concatenate([jnp.full((1, BS), one, jnp.float32) for one in bias], axis=1)
        tokens = slice(b * BS, (b + 1) * BS)
        query = jnp.concatenate(
            [q_ref[tokens, c * head_dim : (c + 1) * head_dim] for c in range(groups)], axis=0
        )
        scores = head_scores(query, block_keys) + bias_row
        if near:
            token = lax.rem(lax.broadcasted_iota(jnp.int32, (groups * BS, LANES), 0), BS)
            key = lax.broadcasted_iota(jnp.int32, (groups * BS, LANES), 1)
            hidden = (key > token) & (key < BS)
            scores = jnp.concatenate(
                [jnp.where(hidden, minus, scores[:, :LANES]), scores[:, LANES:]], axis=1
            )
            top = jnp.max(scores, axis=1, keepdims=True)
            weights = jnp.exp2((scores - top) * factor)
            total = jnp.sum(weights, axis=1, keepdims=True)
            mixed = jnp.dot(
                weights.astype(jnp.bfloat16), block_values, preferred_element_type=jnp.float32
            )
            mixed = mixed / total
            lse = top * factor + jnp.log2(total)
            lanes = lax.broadcasted_iota(jnp.int32, (BS, LANES), 1)
            packed = jnp.zeros((BS, LANES), jnp.float32)
            for c in range(groups):
                part = slice(c * BS, (c + 1) * BS)
                out_ref[tokens, c * head_dim : (c + 1) * head_dim] = mixed[part]
                packed = jnp.where(lanes == c, lse[part], packed)
            lse_ref[0, tokens] = packed
        else:
            before = jnp.concatenate(
                [prev_lse_ref[0, tokens, c : c + 1] for c in range(groups)], axis=0
            )
            top = jnp.maximum(jnp.max(scores, axis=1, keepdims=True) * factor, before)
            weights = jnp.exp2(scores * factor - top)
            share = jnp.exp2(before - top)
            total = jnp.sum(weights, axis=1, keepdims=True) + share
            mixed = jnp.dot(
                weights.astype(jnp.bfloat16), block_values, preferred_element_type=jnp.float32
            )
            inverse = 1.0 / total
            share = share * inverse
            for c in range(groups):
                part = slice(c * BS, (c + 1) * BS)
                cols = slice(c * head_dim, (c + 1) * head_dim)
                merged = mixed[part] * inverse[part] + prev_ref[tokens, cols] * share[part]
                out_ref[tokens, cols] = merged.astype(out_ref.dtype)


def attend(query, key_pieces, value_pieces, vertical, slash, previous, first, where):
    near = previous is None
    pieces = len(key_pieces)
    length, width = query.shape
    heads = vertical.shape[0]
    head_dim = key_pieces[0].shape[1] // heads
    cols = width // heads
    rows = key_pieces[0].shape[0]
    keys_per_block = (slash if near else vertical).shape[1] * BS
    wide = pl.BlockSpec((length, cols), lambda g: (0, g))
    stat = pl.BlockSpec((1, length, LANES), lambda g: (g, 0, 0))
    raw = pl.BlockSpec(memory_space=pl.ANY)
    table = pl.BlockSpec(memory_space=pltpu.SMEM)
    in_specs = [table, table, wide] + [raw] * (2 * pieces)
    operands = [vertical, slash, query, *key_pieces, *value_pieces]
    if near:
        out_shape = (
            jax.ShapeDtypeStruct((length, width), jnp.float32),
            jax.ShapeDtypeStruct((heads, length, LANES), jnp.float32),
        )
        out_specs = (wide, stat)
    else:
        in_specs += [wide, stat]
        operands += list(previous)
        out_shape = jax.ShapeDtypeStruct((length, width), query.dtype)
        out_specs = wide
    work = length * width * keys_per_block
    return pl.pallas_call(
        functools.partial(attend_kernel, (pieces, first, where, near, not near)),
        grid=(heads,),
        in_specs=in_specs,
        out_specs=out_specs,
        out_shape=out_shape,
        scratch_shapes=[
            pltpu.VMEM((2, pieces * rows, head_dim), jnp.bfloat16),
            pltpu.VMEM((2, pieces * rows, head_dim), jnp.bfloat16),
            pltpu.SemaphoreType.DMA((2, 2)),
        ],
        cost_estimate=pl.CostEstimate(
            flops=4 * work, transcendentals=work // head_dim, bytes_accessed=length * width * 8
        ),
        name="attend_near" if near else "attend_far",
    )(*operands)


def gathered(keys, values):
    rows = lax.axis_size("seq") // 2
    forward = lambda block: passed_along(block, "seq", 2)
    levels = []
    own = [keys, values]
    for level in range(rows):
        if level:
            own = [forward(t) for t in own]
        side = [swapped(t, "seq") for t in own[:1]]
        if level == rows - 1 and level:
            side.append(forward(levels[-1][2][1]))
        else:
            side.append(swapped(own[1], "seq"))
        levels.append(
            [own, [swapped(t, "head") for t in own], side, [swapped(t, "head") for t in side]]
        )
    return levels


def row_places(level_count):
    def places():
        inner = lax.rem(lax.axis_index("seq"), 2) * 2 + lax.axis_index("head")
        return [
            (level_count - 1 - level) * 4 + (inner ^ other)
            for level in range(level_count)
            for other in range(4)
        ]

    return places


def owned_columns(here, vertical, first_block):
    count = here.shape[0] // BS
    heads, columns = vertical.shape
    head_dim = here.shape[1] // heads
    blocks = here.reshape(count, BS, heads, head_dim)
    offset = vertical - first_block
    inside = ((offset >= 0) & (offset < count)).T[:, None, :, None]
    total = jnp.zeros((columns, BS, heads, head_dim), here.dtype)
    for n in range(count):
        total = total + jnp.where(
            inside & (offset == n).T[:, None, :, None], blocks[n][None], jnp.zeros((), here.dtype)
        )
    return total.reshape(columns * BS, heads * head_dim)


def on_device(query, keys, values, vertical, slash):
    length = query.shape[0]
    blocks = length // BS
    seq, cores = lax.axis_size("seq"), lax.axis_size("head")
    position = lambda: lax.axis_index("seq") * cores + lax.axis_index("head")
    reach = SPAN - 1
    whole = 2 * seq * cores * keys.size * keys.dtype.itemsize
    if seq % 2 == 0 and cores == 2 and whole <= GATHER_BYTES:
        levels = gathered(keys, values)
        row_blocks = 4 * blocks
        close = min(1 + -(-reach // row_blocks), len(levels))
        row_first = lambda count: lambda: (lax.axis_index("seq") // 2 - (count - 1)) * row_blocks
        flat = [piece for level in levels for piece in level]
        near, far = flat[: 4 * close], flat
        near_first, near_where = row_first(close), row_places(close)
        far_first, far_where = row_first(len(levels)), row_places(len(levels))
    else:
        back = -(-(reach * BS) // length)
        near = [
            [passed_along(t, ("seq", "head"), d) if d else t for t in (keys, values)]
            for d in range(back, -1, -1)
        ]
        near_first = lambda: (position() - back) * blocks
        near_where = lambda: list(range(back + 1))
        first_block = position() * blocks
        far = [
            lax.psum(owned_columns(t, vertical, first_block), ("seq", "head"))
            for t in (keys, values)
        ]
        far = [far]
        far_first = lambda: None
        far_where = lambda: [0]
    split = lambda pieces: ([p[0] for p in pieces], [p[1] for p in pieces])
    previous = attend(query, *split(near), vertical, slash, None, near_first, near_where)
    return attend(query, *split(far), vertical, slash, previous, far_first, far_where)


def solution(mesh):
    in_specs = (
        P(("parts", "seq", "head"), None),
        P(("parts", "seq", "head"), None),
        P(("parts", "seq", "head"), None),
        P("parts", None),
        P("parts", None),
    )
    out_specs = P(("parts", "seq", "head"), None)
    return jax.shard_map(
        on_device, mesh=mesh, in_specs=in_specs, out_specs=out_specs, check_vma=False
    )
```

```python
import functools
import math

import jax
import jax.numpy as jnp
from jax import lax
from jax.experimental import pallas as pl
from jax.experimental.pallas import tpu as pltpu
from jax.sharding import PartitionSpec as P

BS = 64
SPAN = 8
GATHER_BYTES = 16 * 2**20
VMEM_BYTES = 24 * 2**20


def passed_along(block, axis, distance):
    devices = range(lax.axis_size(axis))
    route = [(i - distance, i) for i in devices if i - distance in devices]
    return lax.ppermute(block, axis, route)


def swapped(block, axis):
    return lax.ppermute(block, axis, [(i, i ^ 1) for i in range(lax.axis_size(axis))])


def dot_last(left, right):
    return lax.dot_general(
        left, right, (((1,), (1,)), ((), ())), preferred_element_type=jnp.float32
    )


def folded(reduce, part):
    return reduce(part.reshape(-1, 8, part.shape[1]), axis=0)


def attend_kernel(cfg, *refs):
    pieces, where, near, last, columns = cfg
    slot_ref, bias_ref, q_ref = refs[:3]
    refs = refs[3:]
    key_pieces, value_pieces = refs[:pieces], refs[pieces : 2 * pieces]
    refs = refs[2 * pieces :]
    if not near:
        prev_ref, prev_stat_ref = refs[:2]
        refs = refs[2:]
    if last:
        out_ref, keys, values, sems = refs
    else:
        out_ref, stat_ref, keys, values, sems = refs
    head = pl.program_id(0)
    rows = key_pieces[0].shape[0]
    blocks = q_ref.shape[0] // BS
    head_dim = keys.shape[1] // pl.num_programs(0)
    groups = q_ref.shape[1] // head_dim
    places = where()

    @pl.when(head == 0)
    def _():
        for store, sources, sem in ((keys, key_pieces, 0), (values, value_pieces, 1)):
            for piece in range(pieces):
                to = pl.ds(pl.multiple_of(places[piece] * rows, rows), rows)
                pltpu.make_async_copy(sources[piece], store.at[to], sems.at[sem]).start()
        pltpu.make_async_copy(keys, keys, sems.at[0]).wait()
        pltpu.make_async_copy(values, values, sems.at[1]).wait()

    lanes = pl.ds(pl.multiple_of(head * head_dim, head_dim), head_dim)
    factor = math.log2(math.e) / math.sqrt(head_dim)
    minus = jnp.float32(-jnp.inf)

    def tile(store, at):
        return store[pl.ds(pl.multiple_of(at * BS, BS), BS), lanes]

    def run(picked, bias):
        halves = 2 if groups % 2 == 0 else 1
        part_groups = groups // halves
        width = part_groups * BS
        shared = all(one is picked[0] for one in picked)
        loaded = []
        for b in range(1 if shared else blocks):
            loaded.append(
                (
                    jnp.concatenate([tile(keys, at) for at in picked[b]], axis=0),
                    jnp.concatenate([tile(values, at) for at in picked[b]], axis=0).T,
                )
            )
        loaded = loaded * (blocks if shared else 1)
        units = [(b, h) for b in range(blocks) for h in range(halves)]

        def scores_of(unit):
            b, h = unit
            tokens = slice(b * BS, (b + 1) * BS)
            query = jnp.concatenate(
                [
                    q_ref[tokens, c * head_dim : (c + 1) * head_dim]
                    for c in range(h * part_groups, (h + 1) * part_groups)
                ],
                axis=0,
            )
            return dot_last(loaded[b][0], query)

        def finish(unit, scores):
            b, h = unit
            cols = slice(h * width, (h + 1) * width)
            parts = [scores[m * BS : (m + 1) * BS] for m in range(len(picked[b]))]
            if near:
                key = lax.broadcasted_iota(jnp.int32, (BS, width), 0)
                token = lax.rem(lax.broadcasted_iota(jnp.int32, (BS, width), 1), BS)
                parts[0] = jnp.where(key > token, minus, parts[0])
            tops = [folded(jnp.max, part) + one for part, one in zip(parts, bias[b])]
            top = jnp.max(functools.reduce(jnp.maximum, tops), axis=0, keepdims=True) * factor
            if not near:
                before = prev_stat_ref[0, b, 0:1, cols]
                top = jnp.maximum(top, before)
            weights = [jnp.exp2(part * factor - (top - one)) for part, one in zip(parts, bias[b])]
            total = functools.reduce(jnp.add, [folded(jnp.sum, w) for w in weights])
            total = jnp.sum(total, axis=0, keepdims=True)
            rounded = jnp.concatenate([w.astype(jnp.bfloat16) for w in weights], axis=0)
            mixed = jnp.dot(loaded[b][1], rounded, preferred_element_type=jnp.float32)
            if not near:
                share = jnp.exp2(before - top)
                total = prev_stat_ref[0, b, 1:2, cols] * share + total
            if last:
                inverse = 1.0 / total
                merged = prev_ref[0, b, :, cols] * (share * inverse) + mixed * inverse
                merged = merged.astype(out_ref.dtype).T
                for c in range(part_groups):
                    at = (h * part_groups + c) * head_dim
                    out_ref[b * BS : (b + 1) * BS, at : at + head_dim] = merged[
                        c * BS : (c + 1) * BS
                    ]
            else:
                if not near:
                    mixed = prev_ref[0, b, :, cols] * share + mixed
                out_ref[0, b, :, cols] = mixed
                stat_ref[0, b, 0:1, cols] = top
                stat_ref[0, b, 1:2, cols] = total

        ahead = scores_of(units[0])
        for n, unit in enumerate(units):
            scores = ahead
            if n + 1 < len(units):
                ahead = scores_of(units[n + 1])
            finish(unit, scores)

    def limited(most):
        added = [[bias_ref[head, b * columns + k] for k in range(most)] for b in range(blocks)]
        if near:
            run([[slot_ref[head, b * columns + k] for k in range(most)] for b in range(blocks)], added)
        else:
            run([[slot_ref[head, 1 + k] for k in range(most)]] * blocks, added)

    if near:
        limited(columns)
        return
    count = slot_ref[head, 0]
    steps = list(range(2, columns, 2)) + [columns]
    for low, most in zip([-1] + steps, steps):
        pl.when((count > low) & (count <= most))(functools.partial(limited, most))


def tables_kernel(cfg, *refs):
    stages, blocks = cfg
    vert_ref, slash_ref = refs[:2]
    outs = refs[2:]
    vertical, slash = vert_ref[...], slash_ref[...]
    heads, columns = vertical.shape
    offsets = slash.shape[1]
    lane = lax.broadcasted_iota(jnp.int32, outs[0].shape, 1)
    zeros = jnp.zeros(outs[0].shape, jnp.int32)
    position = lax.axis_index("seq") * lax.axis_size("head") + lax.axis_index("head")

    def column(table, at):
        return table[:, at : at + 1]

    for n, (near, first, slots) in enumerate(stages):
        slot_out, bias_out = zeros, zeros
        first_block = None if first is None else first()
        if near:
            for b in range(blocks):
                for m in range(offsets):
                    offset = column(slash, m)
                    offset = jnp.where(offset == 0, column(slash, 0), offset) if m else 0 * offset
                    wanted = position * blocks + b - offset
                    here = lane == b * offsets + m
                    slot = jnp.clip(wanted - first_block, 0, slots - 1)
                    slot_out = jnp.where(here, slot, slot_out)
                    bias_out = jnp.where(here & (wanted < 0), 1, bias_out)
        else:
            count = jnp.zeros((heads, 1), jnp.int32)
            for m in range(columns):
                wanted = column(vertical, m)
                slot = jnp.full((heads, 1), m, jnp.int32)
                kept = wanted >= 0
                if first_block is not None:
                    slot = wanted - first_block
                    kept = (slot >= 0) & (slot < slots)
                    slot = jnp.clip(slot, 0, slots - 1)
                used = []
                for b in range(blocks):
                    away = position * blocks + b - wanted
                    fresh = kept & (away >= 0)
                    for o in range(offsets):
                        fresh = fresh & (away != column(slash, o))
                    used.append(fresh)
                some = functools.reduce(jnp.logical_or, used)
                slot_out = jnp.where((lane == count + 1) & some, slot, slot_out)
                for b in range(blocks):
                    here = (lane == count + b * columns) & some & used[b]
                    bias_out = jnp.where(here, 1, bias_out)
                count = count + some.astype(jnp.int32)
            bias_out = 1 - bias_out
            slot_out = jnp.where(lane == 0, count, slot_out)
        outs[2 * n][...] = slot_out
        outs[2 * n + 1][...] = jnp.where(bias_out == 1, -jnp.inf, 0.0).astype(jnp.float32)


def make_tables(vertical, slash, blocks, stages):
    heads = vertical.shape[0]
    shapes = []
    for _ in stages:
        shapes += [
            jax.ShapeDtypeStruct((heads, 128), jnp.int32),
            jax.ShapeDtypeStruct((heads, 128), jnp.float32),
        ]
    flat = pl.pallas_call(
        functools.partial(tables_kernel, (stages, blocks)), out_shape=shapes, name="block_tables"
    )(vertical, slash)
    return [flat[2 * n : 2 * n + 2] for n in range(len(stages))]


def attend(query, key_pieces, value_pieces, tables, most, previous, where, last, name):
    near = previous is None
    pieces = len(key_pieces)
    length, width = query.shape
    heads = tables[0].shape[0]
    rows, key_width = key_pieces[0].shape
    head_dim = key_width // heads
    cols = width // heads
    blocks = length // BS
    columns = cols // head_dim * BS
    wide = pl.BlockSpec((length, cols), lambda g: (0, g))
    mixed = pl.BlockSpec((1, blocks, head_dim, columns), lambda g: (g, 0, 0, 0))
    stat = pl.BlockSpec((1, blocks, 8, columns), lambda g: (g, 0, 0, 0))
    raw = pl.BlockSpec(memory_space=pl.ANY)
    table = pl.BlockSpec(memory_space=pltpu.SMEM)
    in_specs = [table, table, wide] + [raw] * (2 * pieces)
    operands = [*tables, query, *key_pieces, *value_pieces]
    if not near:
        in_specs += [mixed, stat]
        operands += list(previous)
    if last:
        out_shape = jax.ShapeDtypeStruct((length, width), query.dtype)
        out_specs = wide
    else:
        out_shape = (
            jax.ShapeDtypeStruct((heads, blocks, head_dim, columns), jnp.float32),
            jax.ShapeDtypeStruct((heads, blocks, 8, columns), jnp.float32),
        )
        out_specs = (mixed, stat)
    work = length * width * most * BS
    return pl.pallas_call(
        functools.partial(attend_kernel, (pieces, where, near, last, most)),
        grid=(heads,),
        in_specs=in_specs,
        out_specs=out_specs,
        out_shape=out_shape,
        scratch_shapes=[
            pltpu.VMEM((pieces * rows, key_width), jnp.bfloat16),
            pltpu.VMEM((pieces * rows, key_width), jnp.bfloat16),
            pltpu.SemaphoreType.DMA((2,)),
        ],
        compiler_params=pltpu.CompilerParams(vmem_limit_bytes=VMEM_BYTES),
        cost_estimate=pl.CostEstimate(
            flops=4 * work, transcendentals=work // head_dim, bytes_accessed=length * width * 8
        ),
        name=name,
    )(*operands)


def gathered(keys, values):
    rows = lax.axis_size("seq") // 2
    forward = lambda block: passed_along(block, "seq", 2)
    levels = []
    own = [keys, values]
    for level in range(rows):
        if level:
            own = [forward(t) for t in own]
        side = [swapped(t, "seq") for t in own[:1]]
        if level == rows - 1 and level:
            side.append(forward(levels[-1][2][1]))
        else:
            side.append(swapped(own[1], "seq"))
        levels.append(
            [own, [swapped(t, "head") for t in own], side, [swapped(t, "head") for t in side]]
        )
    return levels


def row_places(count):
    def places():
        inner = lax.rem(lax.axis_index("seq"), 2) * 2 + lax.axis_index("head")
        return [
            (count - 1 - level) * 4 + (inner ^ other) for level in range(count) for other in range(4)
        ]

    return places


def owned_columns(here, vertical, first_block):
    count = here.shape[0] // BS
    heads, columns = vertical.shape
    head_dim = here.shape[1] // heads
    blocks = here.reshape(count, BS, heads, head_dim)
    offset = vertical - first_block
    inside = ((offset >= 0) & (offset < count)).T[:, None, :, None]
    total = jnp.zeros((columns, BS, heads, head_dim), here.dtype)
    for n in range(count):
        total = total + jnp.where(
            inside & (offset == n).T[:, None, :, None], blocks[n][None], jnp.zeros((), here.dtype)
        )
    return total.reshape(columns * BS, heads * head_dim)


def on_device(query, keys, values, vertical, slash):
    length = query.shape[0]
    blocks = length // BS
    seq, cores = lax.axis_size("seq"), lax.axis_size("head")
    reach = SPAN - 1
    whole = 2 * seq * cores * keys.size * keys.dtype.itemsize
    split = lambda pieces: ([p[0] for p in pieces], [p[1] for p in pieces])
    if seq % 2 == 0 and cores == 2 and whole <= GATHER_BYTES:
        levels = gathered(keys, values)
        row_blocks = 4 * blocks
        close = min(1 + -(-reach // row_blocks), len(levels))
        top = len(levels) - 1
        spans = [(0, close - 1)] + ([(0, top - 1)] if top >= 1 else []) + [(top, top)]

        def from_row(high):
            return lambda: (lax.axis_index("seq") // 2 - high) * row_blocks

        tables = make_tables(
            vertical,
            slash,
            blocks,
            [
                (n == 0, from_row(high), (high - low + 1) * row_blocks)
                for n, (low, high) in enumerate(spans)
            ],
        )
        state = None
        for n, (low, high) in enumerate(spans):
            flat = [piece for level in levels[low : high + 1] for piece in level]
            most = (slash if n == 0 else vertical).shape[1]
            last = n == len(spans) - 1
            name = "attend_near" if n == 0 else "attend_far" if last else "attend_mid"
            places = row_places(high - low + 1)
            state = attend(query, *split(flat), tables[n], most, state, places, last, name)
        return state
    back = -(-(reach * BS) // length)
    near = [
        [passed_along(t, ("seq", "head"), d) if d else t for t in (keys, values)]
        for d in range(back, -1, -1)
    ]
    position = lambda: lax.axis_index("seq") * cores + lax.axis_index("head")
    far = lax.psum(
        tuple(owned_columns(t, vertical, position() * blocks) for t in (keys, values)),
        ("seq", "head"),
    )
    tables = make_tables(
        vertical,
        slash,
        blocks,
        [(True, lambda: (position() - back) * blocks, (back + 1) * blocks), (False, None, 0)],
    )
    places = lambda: list(range(back + 1))
    state = attend(
        query, *split(near), tables[0], slash.shape[1], None, places, False, "attend_near"
    )
    return attend(
        query, [far[0]], [far[1]], tables[1], vertical.shape[1], state, lambda: [0], True, "attend_far"
    )


def solution(mesh):
    in_specs = (
        P(("parts", "seq", "head"), None),
        P(("parts", "seq", "head"), None),
        P(("parts", "seq", "head"), None),
        P("parts", None),
        P("parts", None),
    )
    out_specs = P(("parts", "seq", "head"), None)
    return jax.shard_map(
        on_device, mesh=mesh, in_specs=in_specs, out_specs=out_specs, check_vma=False
    )
```
